256 devices in a mesh: row: 16 (over z, y_hi), col: 16 (over y_lo, x, core).
Axes of the slice: x: 4, y: 4 (y_hi: 2, y_lo: 2; y = y_hi * 2 + y_lo), z: 8, core: 2. Of those that a mesh axis runs over, the one named last changes fastest.
Arguments:
- covariance: float32 [12288, 12288], P('row', 'col'), may hold values from -6 to 6
- blocks: float32 [48, 5, 256, 256], P('col', None, 'row'), may hold values from -0.15625 to 0.15625
- present: int32 [48, 5], replicated, may hold values 0 or 1
- model_noise: float32 [12288, 12288], P('col', 'row'), may hold values from -6 to 6
Outputs:
- forecast: float32 [12288, 12288], P('col', 'row')
The draws below stay inside these ranges and needn't reach their ends.
All inputs are finite; a program needn't handle non-finite values.
Results may differ from the reference program's by a relative error of at most 0.000057.
Values sent between devices are 32-bit elements; how exact they have to be, the bound alone decides.
A program may use at most 128 MiB of HBM per device.

```python
import jax
import jax.numpy as jnp
from jax import lax

N = 12288
BS = 256
NB = 48


def place_ends(values, key, smallest, high):
    longest = values.shape.index(max(values.shape))
    spots = []
    for shift in (0, 1):
        where = [jax.random.randint(jax.random.fold_in(key, axis), (), 0, length) for axis, length in enumerate(values.shape)]
        where[longest] = (where[longest] + shift) % values.shape[longest]
        spots.append(tuple(where))
    return values.at[spots[0]].set(smallest).at[spots[1]].set(high)


def level_of(rng, dims, shards, least, high):
    gain = 1.0
    for dim, parts in shards:
        heights = jax.random.uniform(jax.random.fold_in(jax.random.fold_in(rng, 6), dim), (parts,), jnp.float32, least / len(shards), high / len(shards))
        gain = gain * jnp.repeat(jnp.exp(heights), dims[dim] // parts).reshape((-1,) + (1,) * (len(dims) - 1 - dim))
    return gain


def noise(key, extent, spread, most, pieces=(), kind=jnp.bfloat16):
    array = spread * jax.random.normal(key, extent, jnp.float32)
    if pieces:
        array = array * level_of(key, extent, pieces, -0.22, 0.18)
    return jnp.clip(array, -most, most).astype(kind)


def setup_inputs(seed: int = 0) -> dict:
    seeds = jax.random.split(jax.random.key(seed), 5)
    covariance = noise(seeds[0], (N, N), 1.0, 6.0, ((0, 16), (1, 16)), jnp.float32)
    blocks = noise(seeds[1], (NB, 5, BS, BS), (5 * BS) ** -0.5, 0.15625, ((0, 16), (2, 16)), jnp.float32)
    present = place_ends((jax.random.randint(seeds[2], (NB, 5), 0, 4) < 3).astype(jnp.int32), jax.random.fold_in(seeds[2], 1), 0, 1)
    model_noise = noise(seeds[3], (N, N), 1.0, 6.0, ((0, 16), (1, 16)), jnp.float32)
    return {"covariance": covariance, "blocks": blocks, "present": present, "model_noise": model_noise}


def band_product(live_band, field):
    block_size = live_band.shape[2]
    padded = jnp.pad(field, ((2 * block_size, 2 * block_size), (0, 0)))

    def one_row(pair_item):
        band_row, start = pair_item
        window = lax.dynamic_slice_in_dim(padded, start, 5 * block_size, 0)
        flat_row = jnp.transpose(band_row, (1, 0, 2)).reshape(block_size, 5 * block_size)
        return jnp.dot(flat_row, window, precision=lax.Precision.HIGHEST, preferred_element_type=jnp.float32)

    starts = (jnp.arange(live_band.shape[0]) * block_size).astype(jnp.int32)
    stacked = lax.map(one_row, (live_band, starts))
    return stacked.reshape(-1, field.shape[1])


def reference(covariance, blocks, present, model_noise):
    live_band = blocks * present[:, :, None, None].astype(blocks.dtype)
    mapped = band_product(live_band, covariance)
    return band_product(live_band, mapped.T) + model_noise
```

```python
import functools

import jax
import jax.numpy as jnp
from jax import lax
from jax.experimental import pallas as pl
from jax.experimental.pallas import tpu as pltpu
from jax.sharding import PartitionSpec as P

MESH = pl.DeviceIdType.MESH
F32 = jnp.float32
BF16 = jnp.bfloat16
CHUNKS = 6
WIDE = 128
ORDER = (0, 1, 4, 5, 2, 3)


def split(value):
    high = value.astype(BF16)
    return high, (value - high.astype(F32)).astype(BF16)


def kernel(p_hbm, blk_hbm, pres, q_hbm, out_hbm, win, edge, mrow, mcol, mrow_b, mcol_b, win_b, mapped, halo, bhi, blo, total, ssem, rsem, lsem):
    r = lax.axis_index("row")
    c = lax.axis_index("col")
    z, yh = r // 2, r % 2
    g, k = c // 2, c % 2
    yl, x = g // 4, g % 4

    def at_z(step):
        return ((r + 2 * step + 32) % 16, c)

    def at_x(step):
        return (r, yl * 8 + ((x + step + 4) % 4) * 2 + k)

    partner = (r + 1 - 2 * yh, c)
    mate = (r, c + 1 - 2 * k)
    twin = (r, (c + 8) % 16)
    left = (r, (c + 15) % 16)
    right = (r, (c + 1) % 16)
    turn = lambda n: n + 4 * ((8 - n) // 8)
    there = (c, 2 * ((turn(g) + z) % 8) + yh)
    source_z = (g - turn(z) + 8) % 8
    origin = (2 * source_z + k, r)

    ids = {}

    def ident(name):
        return ids.setdefault(name, len(ids))

    sent = []

    def send(name, src, dst, device):
        n = ident(name)
        copy = pltpu.make_async_remote_copy(src, dst, ssem.at[n], rsem.at[n], device_id=device, device_id_type=MESH)
        copy.start()
        sent.append(copy)

    def arrived(name, dst):
        n = ident(name)
        pltpu.make_async_remote_copy(dst, dst, ssem.at[n], rsem.at[n], device_id=mate, device_id_type=MESH).wait_recv()

    lids = {}

    def local(name, src, dst):
        n = lids.setdefault(name, len(lids))
        copy = pltpu.make_async_copy(src, dst, lsem.at[n])
        copy.start()
        return copy

    def cols(q):
        return pl.ds(q * WIDE, WIDE)

    barrier = pltpu.get_barrier_semaphore()
    peers = (partner, at_z(1), at_z(-1), mate, twin, at_x(1), at_x(-1), at_x(2), left, right, there, origin)
    for peer in peers:
        pl.semaphore_signal(barrier, inc=1, device_id=peer, device_id_type=MESH)
    pl.semaphore_wait(barrier, len(peers))

    slot = k * 8 + x * 2 + yl
    pair = k * 8 + x * 2

    def send_blocks():
        send("col_y", blk_hbm, mcol.at[r], partner)
        g2 = (turn(g) + z) % 8
        send("row_t", blk_hbm, mrow.at[yh * 8 + (g2 % 4) * 2 + g2 // 4], there)

    def send_direct(q):
        send(f"direct{q}", p_hbm.at[pl.ds(256 * (1 - yh), 512), cols(q)], win.at[q, pl.ds(1280 * yh, 512)], partner)

    def send_edge(q):
        send(f"edge{q}", p_hbm.at[pl.ds(512 * yh, 256), cols(q)], edge.at[q], at_z(2 * yh - 1))

    def relay_edge(q):
        arrived(f"edge{q}", edge.at[q])
        send(f"cross{q}", edge.at[q], win.at[q, pl.ds(256 * (5 - 4 * yh), 256)], partner)

    def relay_middle(q):
        arrived(f"direct{q}", win.at[q, pl.ds(0, 512)])
        send(f"middle{q}", win.at[q, pl.ds(1536 * (1 - yh), 256)], win.at[q, pl.ds(1536 * yh, 256)], at_z(1 - 2 * yh))

    major = 1 - 2 * k

    def zpair(n):
        return pl.ds(2 * ((n + 16) % 8), 2)

    def ring_first():
        arrived("col_y", mcol.at[r])
        for name, sign in (("major0", 1), ("minor0", -1)):
            send(name, mcol.at[zpair(z)], mcol.at[zpair(z)], at_z(sign * major))

    def ring_major(t):
        who = zpair(z - major * t)
        arrived(f"major{t - 1}", mcol.at[who])
        if t < 4:
            send(f"major{t}", mcol.at[who], mcol.at[who], at_z(major))

    def ring_minor(t):
        who = zpair(z + major * t)
        arrived(f"minor{t - 1}", mcol.at[who])
        if t < 3:
            send(f"minor{t}", mcol.at[who], mcol.at[who], at_z(-major))

    def row_twin():
        arrived("row_t", mrow.at[slot])
        send("row_y", mrow.at[slot], mrow.at[slot], twin)

    def row_spread():
        arrived("row_y", mrow.at[slot])
        mine = mrow.at[pl.ds(pair, 2)]
        for step in (1, -1, 2):
            send(f"row_x{step}", mine, mine, at_x(step))
        send("row_m0", mine, mine, mate)

    def row_mate(step):
        who = mrow.at[pl.ds(k * 8 + ((x - step + 4) % 4) * 2, 2)]
        arrived(f"row_x{step}", who)
        send(f"row_m{step}", who, who, mate)

    def row_done():
        for step in (0, 1, -1, 2):
            arrived(f"row_m{step}", mrow.at[pl.ds(pair, 2)])

    def flag(b, d, first):
        at = first + b
        inside = at + d - 2
        good = ((inside + 48) // 48) * ((95 - inside) // 48)
        good = good - (good // 2) * good
        return (pres[at, d] * good).astype(F32)

    def convert(src, dst, first, place):
        flags = [[flag(b, d, first) for d in range(5)] for b in range(3)]

        @pl.loop(0, 16)
        def _(s):
            row = place(s)
            for b in range(3):
                for d in range(5):
                    high, low = split(src[s, b, d] * flags[b][d])
                    dst[b, pl.ds(pl.multiple_of(row * 16, 16), 16), d * 256 : (d + 1) * 256] = high
                    dst[b, pl.ds(pl.multiple_of(256 + row * 16, 16), 16), d * 256 : (d + 1) * 256] = low

    def row_place(s):
        g2 = 4 * (s % 2) + (s % 8) // 2
        return 2 * ((g2 - turn(z) + 8) % 8) + s // 8

    def stage_one(q):
        arrived(f"cross{q}", edge.at[q])
        arrived(f"middle{q}", edge.at[q])

        @pl.loop(0, 7)
        def _(t):
            rows = pl.ds(pl.multiple_of(t * 256, 256), 256)
            high, low = split(win[q, rows])
            win_b[rows, 0:WIDE] = high
            win_b[rows, WIDE : 2 * WIDE] = low

        @pl.loop(0, 3)
        def _(i):
            rows = pl.ds(pl.multiple_of(i * 256, 256), 256)
            part = jnp.dot(mrow_b[i], win_b[pl.ds(pl.multiple_of(i * 256, 256), 1280), :], preferred_element_type=F32)
            part = part[:256] + part[256:]
            part = part[:, :WIDE] + part[:, WIDE:]
            mapped[q, rows] = part
            high, low = split(part)
            bhi[rows, 512 + q * WIDE : 512 + (q + 1) * WIDE] = high
            blo[rows, 512 + q * WIDE : 512 + (q + 1) * WIDE] = low

        if q < 4:
            send(f"left{q}", mapped.at[q], halo.at[4 + q], left)
        if q > 1:
            send(f"right{q}", mapped.at[q], halo.at[q - 2], right)

    def take_halo(n):
        if n < 4:
            arrived(f"right{n + 2}", halo.at[n])
            base = n * WIDE
        else:
            arrived(f"left{n - 4}", halo.at[n])
            base = 1280 + (n - 4) * WIDE

        @pl.loop(0, 3)
        def _(i):
            rows = pl.ds(pl.multiple_of(i * 256, 256), 256)
            high, low = split(halo[n, rows])
            bhi[rows, base : base + WIDE] = high
            blo[rows, base : base + WIDE] = low

    def product(i, spot, count):
        d = spot - i
        depth = count * 256
        a = mcol_b[i, :, d * 256 : d * 256 + depth]
        rows = slice(i * 256, (i + 1) * 256)
        dims = (((1,), (1,)), ((), ()))

        @pl.loop(0, 3)
        def _(n):
            these = pl.ds(pl.multiple_of(n * 256, 256), 256)
            one = lax.dot_general(a, bhi[these, spot * 256 : spot * 256 + depth], dims, preferred_element_type=F32)
            two = lax.dot_general(a[:256], blo[these, spot * 256 : spot * 256 + depth], dims, preferred_element_type=F32)
            place = pl.ds(pl.multiple_of(n * 256, 256), 256)
            total[rows, place] += one[:256] + one[256:] + two

    own_blocks = local("blk", blk_hbm, mcol.at[r])
    send_blocks()
    send_direct(ORDER[0])
    send_edge(ORDER[0])
    send_edge(ORDER[1])
    own = [local(f"own{q}", p_hbm.at[:, cols(q)], win.at[q, pl.ds(512, 768)]) for q in ORDER]
    noise = local("noise", q_hbm, total)
    send_direct(ORDER[1])
    relay_edge(ORDER[0])
    own_blocks.wait()
    ring_first()
    for q in ORDER[2:]:
        send_edge(q)
    send_direct(ORDER[2])
    row_twin()
    relay_middle(ORDER[0])
    relay_edge(ORDER[1])
    send_direct(ORDER[3])
    row_spread()
    relay_middle(ORDER[1])
    relay_edge(ORDER[2])
    ring_major(1)
    ring_minor(1)
    send_direct(ORDER[4])
    relay_edge(ORDER[3])
    relay_middle(ORDER[2])
    row_mate(1)
    row_mate(-1)
    send_direct(ORDER[5])
    relay_edge(ORDER[4])
    relay_middle(ORDER[3])
    ring_major(2)
    ring_minor(2)
    row_mate(2)
    relay_edge(ORDER[5])
    relay_middle(ORDER[4])
    row_done()
    convert(mrow, mrow_b, 3 * r, row_place)
    for copy in own:
        copy.wait()
    stage_one(ORDER[0])
    relay_middle(ORDER[5])
    ring_major(3)
    stage_one(ORDER[1])
    ring_minor(3)
    stage_one(ORDER[2])
    stage_one(ORDER[3])
    ring_major(4)
    convert(mcol, mcol_b, 3 * c, lambda s: s)
    noise.wait()
    stage_one(ORDER[4])
    stage_one(ORDER[5])
    for n in (4, 5, 2, 3):
        take_halo(n)
    product(0, 1, 2)
    product(0, 4, 1)
    product(1, 1, 2)
    product(1, 4, 2)
    product(2, 2, 1)
    product(2, 4, 2)
    for n in (0, 1, 6, 7):
        take_halo(n)
    product(0, 0, 1)
    product(0, 3, 1)
    outs = [local("out0", total.at[0:256], out_hbm.at[0:256])]
    product(1, 3, 1)
    outs.append(local("out1", total.at[256:512], out_hbm.at[256:512]))
    product(2, 3, 1)
    product(2, 6, 1)
    outs.append(local("out2", total.at[512:768], out_hbm.at[512:768]))
    for copy in sent:
        copy.wait_send()
    for copy in outs:
        copy.wait()


def body(covariance, blocks, present, model_noise):
    anywhere = pl.BlockSpec(memory_space=pl.ANY)
    return pl.pallas_call(
        kernel,
        out_shape=jax.ShapeDtypeStruct((768, 768), F32),
        in_specs=[anywhere, anywhere, pl.BlockSpec(memory_space=pltpu.SMEM), anywhere],
        out_specs=anywhere,
        scratch_shapes=[
            pltpu.VMEM((CHUNKS, 1792, WIDE), F32),
            pltpu.VMEM((CHUNKS, 256, WIDE), F32),
            pltpu.VMEM((16, 3, 5, 16, 256), F32),
            pltpu.VMEM((16, 3, 5, 16, 256), F32),
            pltpu.VMEM((3, 512, 1280), BF16),
            pltpu.VMEM((3, 512, 1280), BF16),
            pltpu.VMEM((1792, 2 * WIDE), BF16),
            pltpu.VMEM((CHUNKS, 768, WIDE), F32),
            pltpu.VMEM((8, 768, WIDE), F32),
            pltpu.VMEM((768, 1792), BF16),
            pltpu.VMEM((768, 1792), BF16),
            pltpu.VMEM((768, 768), F32),
            pltpu.SemaphoreType.DMA((64,)),
            pltpu.SemaphoreType.DMA((64,)),
            pltpu.SemaphoreType.DMA((16,)),
        ],
        compiler_params=pltpu.CompilerParams(collective_id=0, has_side_effects=True, vmem_limit_bytes=60 << 20),
        name="forecast",
    )(covariance, blocks, present, model_noise)


def solution(mesh):
    in_specs = (P("row", "col"), P("col", None, "row", None), P(), P("col", "row"))
    out_specs = P("col", "row")
    return jax.shard_map(body, mesh=mesh, in_specs=in_specs, out_specs=out_specs, check_vma=False)
```

```python
import functools

import jax
import jax.numpy as jnp
from jax import lax
from jax.experimental import pallas as pl
from jax.experimental.pallas import tpu as pltpu
from jax.sharding import PartitionSpec as P

MESH = pl.DeviceIdType.MESH
F32 = jnp.float32
BF16 = jnp.bfloat16
CHUNKS = 6
PARTS = 4
SEAM = 7
WIDE = 128
ORDER = (0, 1, 4, 5, 2, 3)

SCHEDULE = (
    ("col_y",), ("t1", 0), ("t1", 1), ("t1", 2), ("direct", 0), ("edge", 2), ("ring", 0), ("edge", 0),
    ("edge", 1), ("direct", 1), ("t2", 0), ("t2", 1), ("minor", 0, 1), ("t2", 2), ("major", 0, 1),
    ("cross", 0), ("ring", 1), ("cross", 1), ("direct", 2), ("middle", 0), ("edge", 3), ("ty", 0), ("ty", 1),
    ("major", 0, 2), ("minor", 0, 2), ("ty", 2), ("cross", 2), ("middle", 1), ("direct", 3), ("tx", 0),
    ("major", 1, 1), ("minor", 1, 1), ("middle", 2), ("edge", 4), ("tx", 1), ("tx", 2), ("tf", 0),
    ("cross", 3), ("major", 0, 3), ("minor", 0, 3), ("tf", 1), ("direct", 4), ("tf", 2), ("edge", 5),
    ("major", 1, 2), ("minor", 1, 2), ("tm", 1), ("tm", 0), ("tm", 2), ("cross", 4), ("middle", 3),
    ("direct", 5), ("tc", 0), ("tc", 1), ("tc", 2), ("one", 0), ("major", 0, 4), ("one", 1), ("hop", 0),
    ("major", 1, 3), ("minor", 1, 3), ("cross", 5), ("one", 2), ("hop", 1), ("hop", 2), ("middle", 4),
    ("one", 3), ("major", 1, 4), ("cc",), ("noise",), ("middle", 5), ("hop", 3), ("one", 4), ("take", 4),
    ("take", 5), ("take", 2), ("take", 3), ("prod", 0, 1, 2), ("prod", 0, 4, 1), ("prod", 1, 1, 2), ("hop", 4),
    ("one", 5), ("prod", 1, 4, 2), ("prod", 2, 2, 1), ("prod", 2, 4, 2), ("prod", 0, 3, 1), ("prod", 1, 3, 1),
    ("out", 1), ("hop", 5), ("prod", 2, 3, 1), ("take", 0), ("take", 1), ("prod", 0, 0, 1), ("out", 0),
    ("take", 6), ("take", 7), ("prod", 2, 6, 1), ("out", 2),
)


def split(value):
    high = value.astype(BF16)
    return high, (value - high.astype(F32)).astype(BF16)


def kernel(p_hbm, blk_hbm, pres_hbm, q_hbm, out_hbm, win, edge, hop, detour, mrow, mcol, mrow_b, mcol_b, win_b, mapped, halo, bhi, blo, total, pres, ssem, rsem, lsem):
    r = lax.axis_index("row")
    c = lax.axis_index("col")
    z, yh = r // 2, r % 2
    g, k = c // 2, c % 2
    yl, x = g // 4, g % 4

    def at_z(step):
        return ((r + 2 * step + 32) % 16, c)

    def at_x(step, core):
        return (r, yl * 8 + ((x + step + 8) % 4) * 2 + core)

    partner = (r + 1 - 2 * yh, c)
    mate = (r, c + 1 - 2 * k)
    twin = (r, (c + 8) % 16)
    left = (r, (c + 15) % 16)
    right = (r, (c + 1) % 16)
    first_to, first_from = at_x(z, 1 - k), at_x(-z, 1 - k)
    k0 = 1 - k
    yl_to = (yl + yh + k0) % 2
    core_to = (z // 4 + yl + k0) % 2
    second_to = (2 * (4 * yl + (x - z + 8) % 4) + k0, yl_to * 8 + x * 2 + core_to)

    def held(core, xs, ys):
        return (xs - z % 4 + 4) % 4 + 4 * ((core + z // 4 + yh) % 2), (yh + ys + z // 4) % 2

    z_from, yh_from = held(k, x, yl)
    second_from = (2 * z_from + yh_from, (z // 4) * 8 + x * 2 + 1 - yh)

    ids = {}

    def ident(name):
        return ids.setdefault(name, len(ids))

    def part_rows(part):
        return pl.ds(part * (768 // PARTS), 768 // PARTS)

    sent = []

    def send(name, src, dst, device, when=None):
        n = ident(name)
        copy = pltpu.make_async_remote_copy(src, dst, ssem.at[n], rsem.at[n], device_id=device, device_id_type=MESH)
        if when is None:
            copy.start()
        else:
            pl.when(when)(copy.start)
        sent.append((copy, when))

    def arrived(name, dst):
        n = ident(name)
        pltpu.make_async_remote_copy(dst, dst, ssem.at[n], rsem.at[n], device_id=mate, device_id_type=MESH).wait_recv()

    lids = {}

    def local(name, src, dst):
        n = lids.setdefault(name, len(lids))
        copy = pltpu.make_async_copy(src, dst, lsem.at[n])
        copy.start()
        return copy

    def cols(q):
        return pl.ds(q * WIDE, WIDE)

    own_flags = local("flags", pres_hbm, pres)
    own_blocks = local("blk", blk_hbm, mcol.at[r])
    own = [local(f"own{q}", p_hbm.at[:, cols(q)], win.at[q, pl.ds(512, 768)]) for q in ORDER]
    noise = local("noise", q_hbm, total)

    barrier = pltpu.get_barrier_semaphore()
    peers = (partner, at_z(1), at_z(-1), mate, twin, at_x(1, k), at_x(-1, k), left, right, first_to, first_from, second_to, second_from)
    for peer in peers:
        pl.semaphore_signal(barrier, inc=1, device_id=peer, device_id_type=MESH)
    seam = (c == SEAM) | (c == SEAM + 1)
    helps_right = (yl == 1) & (k == 0) & (x > 0)
    helps_left = (yl == 0) & (k == 1) & (x < 3)
    helps = helps_right | helps_left

    def greet(columns):
        for column in columns:
            pl.semaphore_signal(barrier, inc=1, device_id=(r, column), device_id_type=MESH)

    pl.when(seam)(lambda: greet((1, 3, 5, 10, 12, 14)))
    pl.when(helps)(lambda: greet((SEAM, SEAM + 1)))
    plain = jnp.logical_not(seam | helps)
    pl.when(plain)(lambda: pl.semaphore_wait(barrier, len(peers)))
    pl.when(seam)(lambda: pl.semaphore_wait(barrier, len(peers) + 6))
    pl.when(helps & jnp.logical_not(seam))(lambda: pl.semaphore_wait(barrier, len(peers) + 2))

    slot = k * 8 + x * 2 + yl

    def slot_of(step):
        return k * 8 + ((x + step + 4) % 4) * 2

    def col_y():
        send("col_y", blk_hbm, mcol.at[r], partner)

    def direct(q):
        send(f"direct{q}", p_hbm.at[pl.ds(256 * (1 - yh), 512), cols(q)], win.at[q, pl.ds(1280 * yh, 512)], partner)

    def edge_(q):
        send(f"edge{q}", p_hbm.at[pl.ds(512 * yh, 256), cols(q)], edge.at[q], at_z(2 * yh - 1))

    def cross(q):
        arrived(f"edge{q}", edge.at[q])
        send(f"cross{q}", edge.at[q], win.at[q, pl.ds(256 * (5 - 4 * yh), 256)], partner)

    def middle(q):
        arrived(f"direct{q}", win.at[q, pl.ds(0, 512)])
        send(f"middle{q}", win.at[q, pl.ds(1536 * (1 - yh), 256)], win.at[q, pl.ds(1536 * yh, 256)], at_z(1 - 2 * yh))

    major = 1 - 2 * k

    def level(step, other):
        return 2 * ((z + step + 16) % 8) + (1 - yh if other else yh)

    def ring(other):
        if other:
            arrived("col_y", mcol.at[level(0, 1)])
        src = mcol.at[level(0, 1)] if other else blk_hbm
        for tag, sign in (("major", 1), ("minor", -1)):
            send(f"{tag}{other}_0", src, mcol.at[level(0, other)], at_z(sign * major))

    def major_(other, t):
        who = mcol.at[level(-major * t, other)]
        arrived(f"major{other}_{t - 1}", who)
        if t < 4:
            send(f"major{other}_{t}", who, who, at_z(major))

    def minor_(other, t):
        who = mcol.at[level(major * t, other)]
        arrived(f"minor{other}_{t - 1}", who)
        if t < 3:
            send(f"minor{other}_{t}", who, who, at_z(-major))

    def t1(b):
        send(f"row_a{b}", blk_hbm.at[b], hop.at[b], first_to)

    def t2(b):
        arrived(f"row_a{b}", hop.at[b])
        send(f"row_b{b}", hop.at[b], mrow.at[core_to * 8 + x * 2 + yl_to, b], second_to)

    def ty(b):
        arrived(f"row_b{b}", mrow.at[slot, b])
        send(f"row_y{b}", mrow.at[slot, b], mrow.at[slot, b], twin)

    def pair_at(step, b):
        return mrow.at[pl.ds(slot_of(step), 2), b]

    def tx(b):
        arrived(f"row_y{b}", mrow.at[slot, b])
        mine = pair_at(0, b)
        send(f"row_p{b}", mine, mine, at_x(1, k))
        send(f"row_n{b}", mine, mine, at_x(-1, k))
        send(f"row_m0{b}", mine, mine, mate)

    def tf(b):
        for tag, step, half in (("p", -1, 0), ("n", 1, 1)):
            arrived(f"row_{tag}{b}", pair_at(step, b))
            one = mrow.at[slot_of(step) + half, b]
            send(f"row_{tag}{tag}{b}", one, one, at_x(-step, k))
            send(f"row_m{tag}{b}", pair_at(step, b), pair_at(step, b), mate)

    def tm(b):
        for tag, half in (("p", 0), ("n", 1)):
            one = mrow.at[slot_of(2) + half, b]
            arrived(f"row_{tag}{tag}{b}", one)
            send(f"row_m{tag}{tag}{b}", one, one, mate)

    def td(b):
        for name in ("m0", "mp", "mn"):
            arrived(f"row_{name}{b}", pair_at(0, b))
        for name in ("mpp", "mnn"):
            arrived(f"row_{name}{b}", mrow.at[slot, b])

    def flag(b, d, first):
        at = first + b
        inside = at + d - 2
        good = ((inside + 48) // 48) * ((95 - inside) // 48)
        return (pres[at, d] * good).astype(F32)

    def convert(src, dst, first, place, b):
        flags = [flag(b, d, first) for d in range(5)]

        @pl.loop(0, 16)
        def _(s):
            row = place(s)
            for d in range(5):
                high, low = split(src[s, b, d] * flags[d])
                dst[b, pl.ds(pl.multiple_of(row * 16, 16), 16), d * 256 : (d + 1) * 256] = high
                dst[b, pl.ds(pl.multiple_of(256 + row * 16, 16), 16), d * 256 : (d + 1) * 256] = low

    def row_place(s):
        zs, ys = held(s // 8, (s % 8) // 2, s % 2)
        return 2 * zs + ys

    def tc(b):
        td(b)
        if b == 0:
            own_flags.wait()
        convert(mrow, mrow_b, 3 * r, row_place, b)

    def cc():
        own_blocks.wait()
        for b in range(3):
            convert(mcol, mcol_b, 3 * c, lambda s: s, b)

    def pass_on(side, q, n, when, target, base):
        send(f"{side}_part{q}_0", mapped.at[q, part_rows(0)], halo.at[n, part_rows(0)], (r, target), when)
        for part in range(1, PARTS):
            send(f"{side}_hop{q}_{part}", mapped.at[q, part_rows(part)], detour.at[q], (r, base + 2 * part), when)

    def relay(side, q, n, when, target, part):
        @pl.when(when)
        def _():
            for number in range(1, PARTS):
                @pl.when(part == number)
                def _():
                    arrived(f"{side}_hop{q}_{number}", detour.at[q])
        for number in range(1, PARTS):
            send(f"{side}_part{q}_{number}", detour.at[q], halo.at[n, part_rows(number)], (r, target), when & (part == number))

    def hop_(q):
        if q < 4:
            relay("left", q, 4 + q, helps_left, SEAM, x + 1)
        if q > 1:
            relay("right", q, q - 2, helps_right, SEAM + 1, x)

    def one(q):
        own[ORDER.index(q)].wait()
        arrived(f"cross{q}", edge.at[q])
        arrived(f"middle{q}", edge.at[q])

        @pl.loop(0, 7)
        def _(t):
            rows = pl.ds(pl.multiple_of(t * 256, 256), 256)
            high, low = split(win[q, rows])
            win_b[rows, 0:WIDE] = high
            win_b[rows, WIDE : 2 * WIDE] = low

        @pl.loop(0, 3)
        def _(i):
            rows = pl.ds(pl.multiple_of(i * 256, 256), 256)
            part = jnp.dot(mrow_b[i], win_b[pl.ds(pl.multiple_of(i * 256, 256), 1280), :], preferred_element_type=F32)
            part = part[:256] + part[256:]
            part = part[:, :WIDE] + part[:, WIDE:]
            mapped[q, rows] = part
            high, low = split(part)
            bhi[rows, 512 + q * WIDE : 512 + (q + 1) * WIDE] = high
            blo[rows, 512 + q * WIDE : 512 + (q + 1) * WIDE] = low

        if q < 4:
            send(f"left{q}", mapped.at[q], halo.at[4 + q], left, (c > 0) & (c != SEAM + 1))
            pass_on("left", q, 4 + q, c == SEAM + 1, SEAM, -1)
        if q > 1:
            send(f"right{q}", mapped.at[q], halo.at[q - 2], right, (c < 15) & (c != SEAM))
            pass_on("right", q, q - 2, c == SEAM, SEAM + 1, 8)

    def take(n):
        if n < 4:
            name, base, there = f"right{n + 2}", n * WIDE, c > 0
        else:
            name, base, there = f"left{n - 4}", 1280 + (n - 4) * WIDE, c < 15

        @pl.when(there)
        def _():
            split_up = c == (SEAM + 1 if n < 4 else SEAM)
            pl.when(jnp.logical_not(split_up))(lambda: arrived(name, halo.at[n]))

            @pl.when(split_up)
            def _():
                for part in range(PARTS):
                    arrived(f"{name[:-1]}_part{name[-1]}_{part}", halo.at[n, part_rows(part)])

            @pl.loop(0, 3)
            def _(i):
                rows = pl.ds(pl.multiple_of(i * 256, 256), 256)
                high, low = split(halo[n, rows])
                bhi[rows, base : base + WIDE] = high
                blo[rows, base : base + WIDE] = low

        @pl.when(jnp.logical_not(there))
        def _():
            bhi[:, base : base + WIDE] = jnp.zeros((768, WIDE), BF16)
            blo[:, base : base + WIDE] = jnp.zeros((768, WIDE), BF16)

    def prod(i, spot, count):
        d = spot - i
        depth = count * 256
        a = mcol_b[i, :, d * 256 : d * 256 + depth]
        rows = slice(i * 256, (i + 1) * 256)
        dims = (((1,), (1,)), ((), ()))

        @pl.loop(0, 3)
        def _(n):
            these = pl.ds(pl.multiple_of(n * 256, 256), 256)
            first = lax.dot_general(a, bhi[these, spot * 256 : spot * 256 + depth], dims, preferred_element_type=F32)
            second = lax.dot_general(a[:256], blo[these, spot * 256 : spot * 256 + depth], dims, preferred_element_type=F32)
            total[rows, these] += first[:256] + first[256:] + second

    outs = []

    def out(i):
        outs.append(local(f"out{i}", total.at[i * 256 : (i + 1) * 256], out_hbm.at[i * 256 : (i + 1) * 256]))

    actions = dict(col_y=col_y, direct=direct, edge=edge_, cross=cross, middle=middle, ring=ring, major=major_, minor=minor_, t1=t1, t2=t2, ty=ty, tx=tx, tf=tf, tm=tm, tc=tc, cc=cc, one=one, hop=hop_, take=take, prod=prod, out=out, noise=noise.wait)
    for word, *numbers in SCHEDULE:
        if word in ("direct", "edge", "cross", "middle", "one", "hop"):
            numbers = [ORDER[n] for n in numbers]
        actions[word](*numbers)
    for copy, when in sent:
        if when is None:
            copy.wait_send()
        else:
            pl.when(when)(copy.wait_send)
    for copy in outs:
        copy.wait()


def body(covariance, blocks, present, model_noise):
    anywhere = pl.BlockSpec(memory_space=pl.ANY)
    return pl.pallas_call(
        kernel,
        out_shape=jax.ShapeDtypeStruct((768, 768), F32),
        in_specs=[anywhere] * 4,
        out_specs=anywhere,
        scratch_shapes=[
            pltpu.VMEM((CHUNKS, 1792, WIDE), F32),
            pltpu.VMEM((CHUNKS, 256, WIDE), F32),
            pltpu.VMEM((3, 5, 16, 256), F32),
            pltpu.VMEM((CHUNKS, 768 // PARTS, WIDE), F32),
            pltpu.VMEM((16, 3, 5, 16, 256), F32),
            pltpu.VMEM((16, 3, 5, 16, 256), F32),
            pltpu.VMEM((3, 512, 1280), BF16),
            pltpu.VMEM((3, 512, 1280), BF16),
            pltpu.VMEM((1792, 2 * WIDE), BF16),
            pltpu.VMEM((CHUNKS, 768, WIDE), F32),
            pltpu.VMEM((8, 768, WIDE), F32),
            pltpu.VMEM((768, 1792), BF16),
            pltpu.VMEM((768, 1792), BF16),
            pltpu.VMEM((768, 768), F32),
            pltpu.SMEM((48, 5), jnp.int32),
            pltpu.SemaphoreType.DMA((140,)),
            pltpu.SemaphoreType.DMA((140,)),
            pltpu.SemaphoreType.DMA((16,)),
        ],
        compiler_params=pltpu.CompilerParams(collective_id=0, has_side_effects=True, vmem_limit_bytes=60 << 20),
        name="forecast",
    )(covariance, blocks, present, model_noise)


def solution(mesh):
    in_specs = (P("row", "col"), P("col", None, "row", None), P(), P("col", "row"))
    out_specs = P("col", "row")
    return jax.shard_map(body, mesh=mesh, in_specs=in_specs, out_specs=out_specs, check_vma=False)
```

```python
import functools

import jax
import jax.numpy as jnp
from jax import lax
from jax.experimental import pallas as pl
from jax.experimental.pallas import tpu as pltpu
from jax.sharding import PartitionSpec as P

MESH = pl.DeviceIdType.MESH
F32 = jnp.float32
BF16 = jnp.bfloat16
CHUNKS = 6
PARTS = 4
SEAM = 7
WIDE = 128
ORDER = (0, 1, 4, 5, 2, 3)

SCHEDULE = (
    ("col_y",), ("t1", 0), ("t1", 1), ("t1", 2), ("direct", 0), ("edge", 2), ("ring", 0), ("edge", 0),
    ("edge", 1), ("direct", 1), ("t2", 0), ("t2", 1), ("minor", 0, 1), ("t2", 2), ("major", 0, 1),
    ("cross", 0), ("ring", 1), ("cross", 1), ("direct", 2), ("middle", 0), ("edge", 3), ("ty", 0), ("ty", 1),
    ("major", 0, 2), ("minor", 0, 2), ("ty", 2), ("cross", 2), ("middle", 1), ("direct", 3), ("tx", 0),
    ("major", 1, 1), ("minor", 1, 1), ("middle", 2), ("edge", 4), ("tx", 1), ("tx", 2), ("tf", 0),
    ("cross", 3), ("major", 0, 3), ("minor", 0, 3), ("tf", 1), ("direct", 4), ("tf", 2), ("edge", 5),
    ("major", 1, 2), ("minor", 1, 2), ("tm", 1), ("tm", 0), ("tm", 2), ("cross", 4), ("middle", 3),
    ("direct", 5), ("tc", 0), ("tc", 1), ("tc", 2), ("one", 0), ("major", 0, 4), ("one", 1), ("hop", 0),
    ("major", 1, 3), ("minor", 1, 3), ("cross", 5), ("one", 2), ("hop", 1), ("hop", 2), ("middle", 4),
    ("one", 3), ("major", 1, 4), ("cc",), ("noise",), ("middle", 5), ("hop", 3), ("one", 4), ("take", 4),
    ("take", 5), ("take", 2), ("take", 3), ("prod", 0, 1, 2), ("prod", 0, 4, 1), ("prod", 1, 1, 2), ("hop", 4),
    ("one", 5), ("prod", 1, 4, 2), ("prod", 2, 2, 1), ("prod", 2, 4, 2), ("prod", 0, 3, 1), ("prod", 1, 3, 1),
    ("out", 1), ("hop", 5), ("prod", 2, 3, 1), ("take", 0), ("take", 1), ("prod", 0, 0, 1), ("out", 0),
    ("take", 6), ("take", 7), ("prod", 2, 6, 1), ("out", 2),
)


def split(value):
    high = value.astype(BF16)
    return high, (value - high.astype(F32)).astype(BF16)


def kernel(p_hbm, blk_hbm, pres_hbm, q_hbm, out_hbm, win, edge, hop, detour, mrow, mcol, mrow_b, mcol_b, win_b, mapped, halo, bhi, blo, total, pres, ssem, rsem, lsem):
    r = lax.axis_index("row")
    c = lax.axis_index("col")
    z, yh = r // 2, r % 2
    g, k = c // 2, c % 2
    yl, x = g // 4, g % 4

    def at_z(step):
        return ((r + 2 * step + 32) % 16, c)

    def at_x(step, core):
        return (r, yl * 8 + ((x + step + 8) % 4) * 2 + core)

    partner = (r + 1 - 2 * yh, c)
    mate = (r, c + 1 - 2 * k)
    twin = (r, (c + 8) % 16)
    left = (r, (c + 15) % 16)
    right = (r, (c + 1) % 16)
    first_to, first_from = at_x(z, 1 - k), at_x(-z, 1 - k)
    k0 = 1 - k
    yl_to = (yl + yh + k0) % 2
    core_to = (z // 4 + yl + k0) % 2
    second_to = (2 * (4 * yl + (x - z + 8) % 4) + k0, yl_to * 8 + x * 2 + core_to)

    def held(core, xs, ys):
        return (xs - z % 4 + 4) % 4 + 4 * ((core + z // 4 + yh) % 2), (yh + ys + z // 4) % 2

    z_from, yh_from = held(k, x, yl)
    second_from = (2 * z_from + yh_from, (z // 4) * 8 + x * 2 + 1 - yh)

    ids = {}

    def ident(name):
        return ids.setdefault(name, len(ids))

    def part_rows(part):
        return pl.ds(part * (768 // PARTS), 768 // PARTS)

    sent = []

    def send(name, src, dst, device, when=None):
        n = ident(name)
        copy = pltpu.make_async_remote_copy(src, dst, ssem.at[n], rsem.at[n], device_id=device, device_id_type=MESH)
        if when is None:
            copy.start()
        else:
            pl.when(when)(copy.start)
        sent.append((copy, when))

    def arrived(name, dst):
        n = ident(name)
        pltpu.make_async_remote_copy(dst, dst, ssem.at[n], rsem.at[n], device_id=mate, device_id_type=MESH).wait_recv()

    lids = {}

    def local(name, src, dst):
        n = lids.setdefault(name, len(lids))
        copy = pltpu.make_async_copy(src, dst, lsem.at[n])
        copy.start()
        return copy

    def cols(q):
        return pl.ds(q * WIDE, WIDE)

    own_flags = local("flags", pres_hbm, pres)
    own_blocks = local("blk", blk_hbm, mcol.at[r])
    own = [local(f"own{q}", p_hbm.at[:, cols(q)], win.at[q, pl.ds(512, 768)]) for q in ORDER]
    noise = local("noise", q_hbm, total)

    barrier = pltpu.get_barrier_semaphore()
    peers = (partner, at_z(1), at_z(-1), mate, twin, at_x(1, k), at_x(-1, k), left, right, first_to, first_from, second_to, second_from)
    for peer in peers:
        pl.semaphore_signal(barrier, inc=1, device_id=peer, device_id_type=MESH)
    seam = (c == SEAM) | (c == SEAM + 1)
    helps_right = (yl == 1) & (k == 0) & (x > 0)
    helps_left = (yl == 0) & (k == 1) & (x < 3)
    helps = helps_right | helps_left

    def greet(columns):
        for column in columns:
            pl.semaphore_signal(barrier, inc=1, device_id=(r, column), device_id_type=MESH)

    pl.when(seam)(lambda: greet((1, 3, 5, 10, 12, 14)))
    pl.when(helps)(lambda: greet((SEAM, SEAM + 1)))
    plain = jnp.logical_not(seam | helps)
    pl.when(plain)(lambda: pl.semaphore_wait(barrier, len(peers)))
    pl.when(seam)(lambda: pl.semaphore_wait(barrier, len(peers) + 6))
    pl.when(helps & jnp.logical_not(seam))(lambda: pl.semaphore_wait(barrier, len(peers) + 2))

    slot = k * 8 + x * 2 + yl

    def slot_of(step):
        return k * 8 + ((x + step + 4) % 4) * 2

    def col_y():
        send("col_y", blk_hbm, mcol.at[r], partner)

    def direct(q):
        send(f"direct{q}", p_hbm.at[pl.ds(256 * (1 - yh), 512), cols(q)], win.at[q, pl.ds(1280 * yh, 512)], partner)

    def edge_(q):
        send(f"edge{q}", p_hbm.at[pl.ds(512 * yh, 256), cols(q)], edge.at[q], at_z(2 * yh - 1))

    def cross(q):
        arrived(f"edge{q}", edge.at[q])
        send(f"cross{q}", edge.at[q], win.at[q, pl.ds(256 * (5 - 4 * yh), 256)], partner)

    def middle(q):
        arrived(f"direct{q}", win.at[q, pl.ds(0, 512)])
        send(f"middle{q}", win.at[q, pl.ds(1536 * (1 - yh), 256)], win.at[q, pl.ds(1536 * yh, 256)], at_z(1 - 2 * yh))

    major = 1 - 2 * k

    def level(step, other):
        return 2 * ((z + step + 16) % 8) + (1 - yh if other else yh)

    def ring(other):
        if other:
            arrived("col_y", mcol.at[level(0, 1)])
        src = mcol.at[level(0, 1)] if other else blk_hbm
        for tag, sign in (("major", 1), ("minor", -1)):
            send(f"{tag}{other}_0", src, mcol.at[level(0, other)], at_z(sign * major))

    def major_(other, t):
        who = mcol.at[level(-major * t, other)]
        arrived(f"major{other}_{t - 1}", who)
        if t < 4:
            send(f"major{other}_{t}", who, who, at_z(major))

    def minor_(other, t):
        who = mcol.at[level(major * t, other)]
        arrived(f"minor{other}_{t - 1}", who)
        if t < 3:
            send(f"minor{other}_{t}", who, who, at_z(-major))

    def t1(b):
        send(f"row_a{b}", blk_hbm.at[b], hop.at[b], first_to)

    def t2(b):
        arrived(f"row_a{b}", hop.at[b])
        send(f"row_b{b}", hop.at[b], mrow.at[core_to * 8 + x * 2 + yl_to, b], second_to)

    def ty(b):
        arrived(f"row_b{b}", mrow.at[slot, b])
        send(f"row_y{b}", mrow.at[slot, b], mrow.at[slot, b], twin)

    def pair_at(step, b):
        return mrow.at[pl.ds(slot_of(step), 2), b]

    def tx(b):
        arrived(f"row_y{b}", mrow.at[slot, b])
        mine = pair_at(0, b)
        send(f"row_p{b}", mine, mine, at_x(1, k))
        send(f"row_n{b}", mine, mine, at_x(-1, k))
        send(f"row_m0{b}", mine, mine, mate)

    def tf(b):
        for tag, step, half in (("p", -1, 0), ("n", 1, 1)):
            arrived(f"row_{tag}{b}", pair_at(step, b))
            one = mrow.at[slot_of(step) + half, b]
            send(f"row_{tag}{tag}{b}", one, one, at_x(-step, k))
            send(f"row_m{tag}{b}", pair_at(step, b), pair_at(step, b), mate)

    def tm(b):
        for tag, half in (("p", 0), ("n", 1)):
            one = mrow.at[slot_of(2) + half, b]
            arrived(f"row_{tag}{tag}{b}", one)
            send(f"row_m{tag}{tag}{b}", one, one, mate)

    def td(b):
        for name in ("m0", "mp", "mn"):
            arrived(f"row_{name}{b}", pair_at(0, b))
        for name in ("mpp", "mnn"):
            arrived(f"row_{name}{b}", mrow.at[slot, b])

    def flag(b, d, first):
        at = first + b
        inside = at + d - 2
        good = ((inside + 48) // 48) * ((95 - inside) // 48)
        return (pres[at, d] * good).astype(F32)

    def convert(src, dst, first, place, b):
        flags = [flag(b, d, first) for d in range(5)]

        @pl.loop(0, 16)
        def _(s):
            row = place(s)
            for d in range(5):
                high, low = split(src[s, b, d] * flags[d])
                dst[b, pl.ds(pl.multiple_of(row * 16, 16), 16), d * 256 : (d + 1) * 256] = high
                dst[b, pl.ds(pl.multiple_of(256 + row * 16, 16), 16), d * 256 : (d + 1) * 256] = low

    def row_place(s):
        zs, ys = held(s // 8, (s % 8) // 2, s % 2)
        return 2 * zs + ys

    def tc(b):
        td(b)
        if b == 0:
            own_flags.wait()
        convert(mrow, mrow_b, 3 * r, row_place, b)

    def cc():
        own_blocks.wait()
        for b in range(3):
            convert(mcol, mcol_b, 3 * c, lambda s: s, b)

    def pass_on(side, q, n, when, target, base):
        send(f"{side}_part{q}_0", mapped.at[q, part_rows(0)], halo.at[n, part_rows(0)], (r, target), when)
        for part in range(1, PARTS):
            send(f"{side}_hop{q}_{part}", mapped.at[q, part_rows(part)], detour.at[q], (r, base + 2 * part), when)

    def relay(side, q, n, when, target, part):
        @pl.when(when)
        def _():
            for number in range(1, PARTS):
                @pl.when(part == number)
                def _():
                    arrived(f"{side}_hop{q}_{number}", detour.at[q])
        for number in range(1, PARTS):
            send(f"{side}_part{q}_{number}", detour.at[q], halo.at[n, part_rows(number)], (r, target), when & (part == number))

    def hop_(q):
        if q < 4:
            relay("left", q, 4 + q, helps_left, SEAM, x + 1)
        if q > 1:
            relay("right", q, q - 2, helps_right, SEAM + 1, x)

    def one(q):
        own[ORDER.index(q)].wait()
        def narrow(t):
            rows = pl.ds(pl.multiple_of(t * 256, 256), 256)
            high, low = split(win[q, rows])
            win_b[rows, 0:WIDE] = high
            win_b[rows, WIDE : 2 * WIDE] = low

        pl.loop(2, 5)(narrow)
        arrived(f"cross{q}", edge.at[q])
        arrived(f"middle{q}", edge.at[q])
        pl.loop(0, 4)(lambda i: narrow(i + 3 * (i // 2)))

        @pl.loop(0, 3)
        def _(i):
            rows = pl.ds(pl.multiple_of(i * 256, 256), 256)
            part = jnp.dot(mrow_b[i], win_b[pl.ds(pl.multiple_of(i * 256, 256), 1280), :], preferred_element_type=F32)
            part = part[:256] + part[256:]
            part = part[:, :WIDE] + part[:, WIDE:]
            mapped[q, rows] = part
            high, low = split(part)
            bhi[rows, 512 + q * WIDE : 512 + (q + 1) * WIDE] = high
            blo[rows, 512 + q * WIDE : 512 + (q + 1) * WIDE] = low

        if q < 4:
            send(f"left{q}", mapped.at[q], halo.at[4 + q], left, (c > 0) & (c != SEAM + 1))
            pass_on("left", q, 4 + q, c == SEAM + 1, SEAM, -1)
        if q > 1:
            send(f"right{q}", mapped.at[q], halo.at[q - 2], right, (c < 15) & (c != SEAM))
            pass_on("right", q, q - 2, c == SEAM, SEAM + 1, 8)

    def take(n):
        if n < 4:
            name, base, there = f"right{n + 2}", n * WIDE, c > 0
        else:
            name, base, there = f"left{n - 4}", 1280 + (n - 4) * WIDE, c < 15

        @pl.when(there)
        def _():
            split_up = c == (SEAM + 1 if n < 4 else SEAM)
            pl.when(jnp.logical_not(split_up))(lambda: arrived(name, halo.at[n]))

            @pl.when(split_up)
            def _():
                for part in range(PARTS):
                    arrived(f"{name[:-1]}_part{name[-1]}_{part}", halo.at[n, part_rows(part)])

            @pl.loop(0, 3)
            def _(i):
                rows = pl.ds(pl.multiple_of(i * 256, 256), 256)
                high, low = split(halo[n, rows])
                bhi[rows, base : base + WIDE] = high
                blo[rows, base : base + WIDE] = low

        @pl.when(jnp.logical_not(there))
        def _():
            bhi[:, base : base + WIDE] = jnp.zeros((768, WIDE), BF16)
            blo[:, base : base + WIDE] = jnp.zeros((768, WIDE), BF16)

    def prod(i, spot, count):
        d = spot - i
        depth = count * 256
        a = mcol_b[i, :, d * 256 : d * 256 + depth]
        rows = slice(i * 256, (i + 1) * 256)
        dims = (((1,), (1,)), ((), ()))

        @pl.loop(0, 3)
        def _(n):
            these = pl.ds(pl.multiple_of(n * 256, 256), 256)
            first = lax.dot_general(a, bhi[these, spot * 256 : spot * 256 + depth], dims, preferred_element_type=F32)
            second = lax.dot_general(a[:256], blo[these, spot * 256 : spot * 256 + depth], dims, preferred_element_type=F32)
            total[rows, these] += first[:256] + first[256:] + second

    outs = []

    def out(i):
        outs.append(local(f"out{i}", total.at[i * 256 : (i + 1) * 256], out_hbm.at[i * 256 : (i + 1) * 256]))

    actions = dict(col_y=col_y, direct=direct, edge=edge_, cross=cross, middle=middle, ring=ring, major=major_, minor=minor_, t1=t1, t2=t2, ty=ty, tx=tx, tf=tf, tm=tm, tc=tc, cc=cc, one=one, hop=hop_, take=take, prod=prod, out=out, noise=noise.wait)
    for word, *numbers in SCHEDULE:
        if word in ("direct", "edge", "cross", "middle", "one", "hop"):
            numbers = [ORDER[n] for n in numbers]
        actions[word](*numbers)
    for copy, when in sent:
        if when is None:
            copy.wait_send()
        else:
            pl.when(when)(copy.wait_send)
    for copy in outs:
        copy.wait()


def body(covariance, blocks, present, model_noise):
    anywhere = pl.BlockSpec(memory_space=pl.ANY)
    return pl.pallas_call(
        kernel,
        out_shape=jax.ShapeDtypeStruct((768, 768), F32),
        in_specs=[anywhere] * 4,
        out_specs=anywhere,
        scratch_shapes=[
            pltpu.VMEM((CHUNKS, 1792, WIDE), F32),
            pltpu.VMEM((CHUNKS, 256, WIDE), F32),
            pltpu.VMEM((3, 5, 16, 256), F32),
            pltpu.VMEM((CHUNKS, 768 // PARTS, WIDE), F32),
            pltpu.VMEM((16, 3, 5, 16, 256), F32),
            pltpu.VMEM((16, 3, 5, 16, 256), F32),
            pltpu.VMEM((3, 512, 1280), BF16),
            pltpu.VMEM((3, 512, 1280), BF16),
            pltpu.VMEM((1792, 2 * WIDE), BF16),
            pltpu.VMEM((CHUNKS, 768, WIDE), F32),
            pltpu.VMEM((8, 768, WIDE), F32),
            pltpu.VMEM((768, 1792), BF16),
            pltpu.VMEM((768, 1792), BF16),
            pltpu.VMEM((768, 768), F32),
            pltpu.SMEM((48, 5), jnp.int32),
            pltpu.SemaphoreType.DMA((140,)),
            pltpu.SemaphoreType.DMA((140,)),
            pltpu.SemaphoreType.DMA((16,)),
        ],
        compiler_params=pltpu.CompilerParams(collective_id=0, has_side_effects=True, vmem_limit_bytes=60 << 20),
        name="forecast",
    )(covariance, blocks, present, model_noise)


def solution(mesh):
    in_specs = (P("row", "col"), P("col", None, "row", None), P(), P("col", "row"))
    out_specs = P("col", "row")
    return jax.shard_map(body, mesh=mesh, in_specs=in_specs, out_specs=out_specs, check_vma=False)
```
